512 devices in a mesh: band: 16 (over z_hi, x, core), dom: 32 (over z_lo, y).
Axes of the slice: x: 4, y: 4, z: 16 (z_hi: 2, z_lo: 8; z = z_hi * 8 + z_lo), core: 2. Of those that a mesh axis runs over, the one named last changes fastest.
Arguments:
- orbitals: bfloat16 [20, 32, 8, 8, 4096], P(None, 'dom', None, None, 'band'), may hold values from -6 to 6
- rotation: bfloat16 [4096, 4096], P(None, 'band'), may hold values from -0.09375 to 0.09375
- potential: float32 [8, 32, 8, 8], P(None, 'dom'), may hold values from -4 to 4
Outputs:
- filtered: float32 [8, 32, 8, 8, 4096], P(None, 'dom', None, None, 'band')
The draws below stay inside these ranges and needn't reach their ends.
All inputs are finite; a program needn't handle non-finite values.
Results may differ from the reference program's by a relative error of at most 0.0003.
Values may be sent and summed in bfloat16 or wider, within the bound.
No kernel may reach another device: no remote copies, remote signals or barrier semaphores. Data moves between devices by JAX's collectives and lax.ppermute only.
A program may use at most 64 MiB of HBM per device.

```python
import jax
import jax.numpy as jnp
from jax import lax

ORBITALS = 4096
TILE_X = 8
TILE_Y = 8
TILES_Y = 4
PLANES = 8
GHOSTED = 20
TILES = 32
TILES_X = 8
GRID_X = 64
GRID_Y = 32


def draw_orbitals(key, part):
    draw_shape = (GHOSTED, TILES, TILE_X, TILE_Y, ORBITALS)
    values = jnp.clip(jax.random.normal(key, draw_shape, jnp.float32), -6.0, 6.0)
    plane_index = jnp.arange(GHOSTED)
    outer_planes = (plane_index < 2) | (plane_index >= GHOSTED - 2)
    level_scale = jnp.where(outer_planes, 1.0, 2.0 ** (-10)).astype(jnp.float32)
    return (values * level_scale[:, None, None, None, None]).astype(jnp.bfloat16)


def steps_of(stream_key, extent, pieces, least, high):
    factor_of = 1.0
    for axis_at, shards_of in pieces:
        steps = jax.random.uniform(jax.random.fold_in(jax.random.fold_in(stream_key, 6), axis_at), (shards_of,), jnp.float32, least / len(pieces), high / len(pieces))
        factor_of = factor_of * jnp.repeat(jnp.exp(steps), extent[axis_at] // shards_of).reshape((-1,) + (1,) * (len(extent) - 1 - axis_at))
    return factor_of


def noise(key, dims, scale, bound, shards=(), held_as=jnp.bfloat16):
    result = jax.random.normal(key, dims, jnp.float32) * scale
    if len(shards) > 0:
        result = steps_of(key, dims, shards, -0.22, 0.18) * result
    return jnp.clip(result, min=-bound, max=bound).astype(held_as)


def setup_inputs(seed: int = 0) -> dict:
    streams_of = jax.random.split(jax.random.key(seed), 4)
    return {
        "orbitals": draw_orbitals(jax.random.fold_in(streams_of[3], 71), 0),
        "rotation": noise(streams_of[1], (ORBITALS, ORBITALS), ORBITALS ** -0.5, 0.09375, ((1, 16),)),
        "potential": jnp.clip(jax.random.uniform(streams_of[2], (PLANES, TILES, TILE_X, TILE_Y), jnp.float32, -4.0, 4.0) * steps_of(streams_of[2], (PLANES, TILES, TILE_X, TILE_Y), ((1, 32),), -0.4, 0.0), -4.0, 4.0),
    }


stencil_weights = (-5369.0 / 1800.0, 12.0 / 7.0, -15.0 / 56.0, 10.0 / 189.0, -1.0 / 112.0, 2.0 / 1925.0, -1.0 / 16632.0)
inverse_spacing = 4.0
centre_shift = 20.0
spread_scale = 24.0


def to_grid(tiled):
    depth_count = tiled.shape[0]
    trailing = tuple(tiled.shape[4:])
    blocked = tiled.reshape((depth_count, TILES_X, TILES_Y, TILE_X, TILE_Y) + trailing)
    ordering = (0, 1, 3, 2, 4) + tuple(range(5, 5 + len(trailing)))
    return blocked.transpose(ordering).reshape((depth_count, GRID_X, GRID_Y) + trailing)


def to_tiles(whole):
    blocked = whole.reshape(PLANES, TILES_X, TILE_X, TILES_Y, TILE_Y, ORBITALS)
    return blocked.transpose(0, 1, 3, 2, 4, 5).reshape(PLANES, TILES, TILE_X, TILE_Y, ORBITALS)


def filter_block(rotated, potential_grid):
    reach = len(stencil_weights) - 1
    planes = potential_grid.shape[0]
    centre = rotated[reach:reach + planes]
    padded = jnp.pad(centre, ((0, 0), (reach, reach), (reach, reach), (0, 0)))
    accumulated = 3.0 * stencil_weights[0] * centre
    for offset in range(1, reach + 1):
        neighbours = rotated[reach + offset:reach + offset + planes] + rotated[reach - offset:reach - offset + planes]
        neighbours = neighbours + padded[:, reach + offset:reach + offset + GRID_X, reach:reach + GRID_Y]
        neighbours = neighbours + padded[:, reach - offset:reach - offset + GRID_X, reach:reach + GRID_Y]
        neighbours = neighbours + padded[:, reach:reach + GRID_X, reach + offset:reach + offset + GRID_Y]
        neighbours = neighbours + padded[:, reach:reach + GRID_X, reach - offset:reach - offset + GRID_Y]
        accumulated = accumulated + stencil_weights[offset] * neighbours
    hamiltonian = (-0.5 * inverse_spacing) * accumulated + (potential_grid[..., None] - centre_shift) * centre
    return hamiltonian / spread_scale


def reference(orbitals, rotation, potential):
    flattened = to_grid(orbitals).reshape(GHOSTED * GRID_X * GRID_Y, ORBITALS)
    potential_grid = to_grid(potential)
    width_block = min(ORBITALS, 256)
    count_blocks = ORBITALS // width_block
    column_blocks = rotation.reshape(ORBITALS, count_blocks, width_block).transpose(1, 0, 2)

    def one_block(columns_rotation):
        rotated = jnp.dot(flattened, columns_rotation, preferred_element_type=jnp.float32)
        rotated = rotated.reshape(GHOSTED, GRID_X, GRID_Y, width_block)
        return filter_block(rotated, potential_grid)

    stacked = lax.map(one_block, column_blocks)
    whole = stacked.transpose(1, 2, 3, 0, 4).reshape(PLANES, GRID_X, GRID_Y, ORBITALS)
    return to_tiles(whole)
```

```python
import jax
import jax.numpy as jnp
from jax import lax
from jax.sharding import PartitionSpec as P

TILES_Y = 4


stencil_weights = (
    -5369.0 / 1800.0,
    12.0 / 7.0,
    -15.0 / 56.0,
    10.0 / 189.0,
    -1.0 / 112.0,
    2.0 / 1925.0,
    -1.0 / 16632.0,
)
inverse_spacing = 4.0
centre_shift = 20.0
spread_scale = 24.0

HALVES = 2
SIDE = 8
TAIL = 8

side_groups = [[h * SIDE + i for i in range(SIDE)] for h in range(HALVES)]
half_swap = [(b, (b + SIDE) % (HALVES * SIDE)) for b in range(HALVES * SIDE)]


def from_behind(value, axis, steps):
    count = lax.axis_size(axis)
    initial, last = (max(0, -steps), min(count, count - steps))
    return lax.ppermute(value, axis, [(source, source + steps) for source in range(initial, last)])


def along_y(value, steps):
    count = lax.axis_size("dom")
    pairs = [
        (source, source + steps)
        for source in range(count)
        if 0 <= source % TILES_Y + steps < TILES_Y
    ]
    return lax.ppermute(value, "dom", pairs)


def apply_filter(slab_local, potential_local):
    reach = len(stencil_weights) - 1
    planes = potential_local.shape[0]
    extent_first = slab_local.shape[1]
    extent_second = slab_local.shape[2]
    middle = slab_local[reach : reach + planes]
    below_first = from_behind(middle[:, extent_first - reach :], "dom", TILES_Y)
    above_first = from_behind(middle[:, :reach], "dom", -TILES_Y)
    below_second = along_y(middle[:, :, extent_second - reach :], 1)
    above_second = along_y(middle[:, :, :reach], -1)
    wide = jnp.float32
    widened_first = jnp.concatenate([below_first, middle, above_first], axis=1).astype(wide)
    widened_second = jnp.concatenate([below_second, middle, above_second], axis=2).astype(wide)
    slab = slab_local.astype(wide)
    centre = middle.astype(wide)
    accumulated = 3.0 * stencil_weights[0] * centre
    for offset in range(1, reach + 1):
        neighbours = slab[reach + offset : reach + offset + planes]
        neighbours = neighbours + slab[reach - offset : reach - offset + planes]
        neighbours = neighbours + widened_first[:, reach + offset : reach + offset + extent_first]
        neighbours = neighbours + widened_first[:, reach - offset : reach - offset + extent_first]
        neighbours = (
            neighbours + widened_second[:, :, reach + offset : reach + offset + extent_second]
        )
        neighbours = (
            neighbours + widened_second[:, :, reach - offset : reach - offset + extent_second]
        )
        accumulated = accumulated + stencil_weights[offset] * neighbours
    hamiltonian = (
        -0.5 * inverse_spacing * accumulated + (potential_local[..., None] - centre_shift) * centre
    )
    return hamiltonian / spread_scale


def encode(value):
    largest = jnp.max(jnp.abs(value))
    exponent = jnp.floor(jnp.log2(jnp.maximum(largest, 2.0**-100))) - 14.0
    scaled = (value * jnp.exp2(-exponent)).astype(jnp.float16)
    tail = jnp.broadcast_to(exponent.astype(jnp.float16), (TAIL, value.shape[1]))
    return jnp.concatenate([scaled, tail], axis=0)


def spread(code):
    return lax.all_gather(code, "band", axis=0, axis_index_groups=side_groups)


def product(codes, matrix, rows):
    exponent = codes[:, rows : rows + 1, :1].astype(jnp.float32)
    value = codes[:, :rows].astype(jnp.float32) * jnp.exp2(exponent)
    high = lax.reduce_precision(value, 8, 7)
    low = (value - high).astype(jnp.bfloat16)
    high = high.astype(jnp.bfloat16)
    dims = (((0, 2), (0, 1)), ((), ()))
    first = lax.dot_general(high, matrix, dims, preferred_element_type=jnp.float32)
    second = lax.dot_general(low, matrix, dims, preferred_element_type=jnp.float32)
    return first + second


def on_device(orbitals, rotation, potential):
    ghosted = orbitals.shape[0]
    extent_first = orbitals.shape[2]
    extent_second = orbitals.shape[3]
    columns = orbitals.shape[4]
    planes = potential.shape[0]
    new_columns = rotation.shape[1]
    rows = planes * extent_first * extent_second
    slab_local = orbitals.reshape(ghosted, extent_first, extent_second, columns)
    potential_local = potential.reshape(planes, extent_first, extent_second)

    filtered = apply_filter(slab_local, potential_local).reshape(rows, columns)
    code = encode(filtered)
    rotation, code = lax.optimization_barrier((rotation, code))
    half = lax.axis_index("band") // SIDE
    halves = rotation.reshape(HALVES, SIDE, columns, new_columns)
    arrived = lax.ppermute(code, "band", half_swap)
    gathered = spread(code)
    own_matrix = lax.dynamic_index_in_dim(halves, half, 0, keepdims=False)
    own = product(gathered, own_matrix, rows)
    gathered = spread(arrived)
    other_matrix = lax.dynamic_index_in_dim(halves, 1 - half, 0, keepdims=False)
    result = own + product(gathered, other_matrix, rows)
    return result.reshape(planes, 1, extent_first, extent_second, new_columns)


def solution(mesh):
    in_specs = (P(None, "dom", None, None, "band"), P(None, "band"), P(None, "dom", None, None))
    out_specs = P(None, "dom", None, None, "band")
    return jax.shard_map(
        on_device, mesh=mesh, in_specs=in_specs, out_specs=out_specs, check_vma=False
    )
```

```python
import jax
import jax.numpy as jnp
from jax import lax
from jax.experimental import pallas as pl
from jax.experimental.pallas import tpu as pltpu
from jax.sharding import PartitionSpec as P

TILES_Y = 4


stencil_weights = (
    -5369.0 / 1800.0,
    12.0 / 7.0,
    -15.0 / 56.0,
    10.0 / 189.0,
    -1.0 / 112.0,
    2.0 / 1925.0,
    -1.0 / 16632.0,
)
inverse_spacing = 4.0
centre_shift = 20.0
spread_scale = 24.0

HALVES = 2
SIDE = 8
TAIL = 8
KERNEL_VMEM = 12 * 1024 * 1024

side_groups = [[h * SIDE + i for i in range(SIDE)] for h in range(HALVES)]
half_swap = [(b, (b + SIDE) % (HALVES * SIDE)) for b in range(HALVES * SIDE)]


def from_behind(value, axis, steps):
    count = lax.axis_size(axis)
    initial, last = (max(0, -steps), min(count, count - steps))
    return lax.ppermute(value, axis, [(source, source + steps) for source in range(initial, last)])


def along_y(value, steps):
    count = lax.axis_size("dom")
    pairs = [
        (source, source + steps)
        for source in range(count)
        if 0 <= source % TILES_Y + steps < TILES_Y
    ]
    return lax.ppermute(value, "dom", pairs)


def ramp(shape, axis):
    column = lax.broadcasted_iota(jnp.int32, shape, axis)
    return ((column * 159) & 255).astype(jnp.float32) / 256.0


def lateral_weights(extent, sources, place):
    factor = -0.5 * inverse_spacing / spread_scale
    shape = (extent * extent, sources)
    row = lax.broadcasted_iota(jnp.int32, shape, 0)
    first, second = place(lax.broadcasted_iota(jnp.int32, shape, 1))
    first = jnp.abs(row // extent - first)
    second = jnp.abs(row % extent - second)
    apart = jnp.where((first == 0) != (second == 0), first + second, 0)
    weights = jnp.zeros(shape, jnp.float32)
    for offset in range(1, len(stencil_weights)):
        weights = jnp.where(apart == offset, factor * stencil_weights[offset], weights)
    return weights


def store_terms(out_ref, matrix):
    rows = matrix.shape[0]
    for term in range(3):
        part = matrix.astype(jnp.bfloat16)
        out_ref[term * rows : (term + 1) * rows] = part
        matrix = matrix - part.astype(jnp.float32)


def along_planes(slab_ref, potential_ref, out_ref, first_ref, second_ref):
    reach = len(stencil_weights) - 1
    factor = -0.5 * inverse_spacing / spread_scale
    planes, points, columns = out_ref.shape
    extent = potential_ref.shape[1]
    cube = (planes * points // extent, extent, extent)
    across = lax.broadcasted_iota(jnp.int32, cube, 1) == lax.broadcasted_iota(jnp.int32, cube, 2)
    shift = jnp.where(across, jnp.broadcast_to(potential_ref[...][:, None, :], cube), 0.0)
    shift = jnp.sum(shift, axis=2, keepdims=True).reshape(planes, points, 1)
    shift = (shift - centre_shift) / spread_scale + 3.0 * factor * stencil_weights[0]
    width = 128
    for lane in range(0, columns, width):
        part = pl.ds(lane, width)
        for plane in range(planes):
            centre = slab_ref[plane + reach, :, part].astype(jnp.float32)
            total = shift[plane] * centre
            for offset in range(1, reach + 1):
                pair = slab_ref[plane + reach + offset, :, part].astype(jnp.float32)
                pair = pair + slab_ref[plane + reach - offset, :, part].astype(jnp.float32)
                total = total + factor * stencil_weights[offset] * pair
            out_ref[plane, :, part] = total
    halo = reach * extent

    def with_first(number):
        at = number // extent
        at = jnp.where(number >= points, at - extent - reach, at)
        at = jnp.where(number >= points + halo, at + extent, at)
        return at, number % extent

    def with_second(number):
        at = number % points
        return at // extent, at % extent + jnp.where(number < points, -extent, extent)

    store_terms(first_ref, lateral_weights(extent, first_ref.shape[1], with_first))
    store_terms(second_ref, lateral_weights(extent, second_ref.shape[1], with_second))


def lateral(
    partial_ref,
    middle_ref,
    below_first_ref,
    above_first_ref,
    below_second_ref,
    above_second_ref,
    first_ref,
    second_ref,
    out_ref,
):
    planes, points, columns = partial_ref.shape
    halo = above_first_ref.shape[1]
    largest = jnp.zeros((points, columns), jnp.float32)
    for plane in range(planes):
        here = jnp.concatenate(
            [middle_ref[plane], below_first_ref[plane, points - halo :], above_first_ref[plane]],
            axis=0,
        )
        there = jnp.concatenate([below_second_ref[plane], above_second_ref[plane]], axis=0)
        terms = jnp.dot(first_ref[...], here, preferred_element_type=jnp.float32)
        terms = terms + jnp.dot(second_ref[...], there, preferred_element_type=jnp.float32)
        total = partial_ref[plane] + (
            terms[:points] + (terms[points : 2 * points] + terms[2 * points :])
        )
        out_ref[plane * points : (plane + 1) * points] = total
        largest = jnp.maximum(largest, jnp.abs(total))
    largest = jnp.max(jnp.max(largest, axis=0, keepdims=True), axis=1, keepdims=True)
    largest = jnp.broadcast_to(largest, (TAIL, columns))
    exponent = jnp.floor(jnp.log2(jnp.maximum(largest, 2.0**-100))) - 13.0
    factor = jnp.exp2(ramp((TAIL, columns), 1) - exponent)[:1]
    for plane in range(planes):
        block = slice(plane * points, (plane + 1) * points)
        out_ref[block] = out_ref[block] * factor
    out_ref[planes * points :] = exponent


def filtered_code(slab, potential):
    reach = len(stencil_weights) - 1
    planes, extent_first, extent_second = potential.shape
    points, columns = slab.shape[1:]
    middle = slab[reach : reach + planes]
    below_second = along_y(middle, 1)
    above_second = along_y(middle, -1)
    below_first = from_behind(middle, "dom", TILES_Y)
    above_first = from_behind(middle[:, : reach * extent_second], "dom", -TILES_Y)
    vmem = pl.BlockSpec(memory_space=pltpu.VMEM)
    params = pltpu.CompilerParams(vmem_limit_bytes=KERNEL_VMEM)
    halo = reach * extent_second
    values = planes * points * columns
    partial, first, second = pl.pallas_call(
        along_planes,
        out_shape=(
            jax.ShapeDtypeStruct((planes, points, columns), jnp.float32),
            jax.ShapeDtypeStruct((3 * points, points + 2 * halo), jnp.bfloat16),
            jax.ShapeDtypeStruct((3 * points, 2 * points), jnp.bfloat16),
        ),
        in_specs=[vmem] * 2,
        out_specs=(vmem,) * 3,
        cost_estimate=pl.CostEstimate(
            flops=30 * values, bytes_accessed=2 * slab.size + 4 * values, transcendentals=0
        ),
        compiler_params=params,
        name="along_planes",
    )(slab, potential.reshape(planes * extent_first, extent_second))
    scaled = pl.pallas_call(
        lateral,
        out_shape=jax.ShapeDtypeStruct((planes * points + TAIL, columns), jnp.float32),
        in_specs=[vmem] * 8,
        out_specs=vmem,
        cost_estimate=pl.CostEstimate(
            flops=2 * planes * (first.size + second.size) * columns,
            bytes_accessed=16 * values,
            transcendentals=0,
        ),
        compiler_params=params,
        name="lateral",
    )(partial, middle, below_first, above_first, below_second, above_second, first, second)
    return scaled.astype(jnp.float16)


def spread(code):
    return lax.all_gather(code, "band", axis=0, axis_index_groups=side_groups)


def product(codes, matrix, rows, start=None):
    exponent = codes[:, rows : rows + 1].astype(jnp.float32)
    factor = jnp.exp2(exponent - ramp((1, 1, codes.shape[2]), 2))
    value = codes[:, :rows].astype(jnp.float32) * factor
    high = lax.reduce_precision(value, 8, 7)
    low = (value - high).astype(jnp.bfloat16)
    high = high.astype(jnp.bfloat16)
    dims = (((0, 2), (0, 1)), ((), ()))
    first = lax.dot_general(high, matrix, dims, preferred_element_type=jnp.float32)
    second = lax.dot_general(low, matrix, dims, preferred_element_type=jnp.float32)
    return (first if start is None else start + first) + second


def on_device(orbitals, rotation, potential):
    ghosted = orbitals.shape[0]
    extent_first = orbitals.shape[2]
    extent_second = orbitals.shape[3]
    columns = orbitals.shape[4]
    planes = potential.shape[0]
    new_columns = rotation.shape[1]
    rows = planes * extent_first * extent_second
    slab_local = orbitals.reshape(ghosted, extent_first * extent_second, columns)
    potential_local = potential.reshape(planes, extent_first, extent_second)

    code = filtered_code(slab_local, potential_local)
    rotation, code = lax.optimization_barrier((rotation, code))
    half = lax.axis_index("band") // SIDE
    halves = rotation.reshape(HALVES, SIDE, columns, new_columns)
    arrived = lax.ppermute(code, "band", half_swap)
    gathered = spread(code)
    own_matrix = lax.dynamic_index_in_dim(halves, half, 0, keepdims=False)
    own = product(gathered, own_matrix, rows)
    arrived, own = lax.optimization_barrier((arrived, own))
    gathered = spread(arrived)
    other_matrix = lax.dynamic_index_in_dim(halves, 1 - half, 0, keepdims=False)
    result = product(gathered, other_matrix, rows, own)
    return result.reshape(planes, 1, extent_first, extent_second, new_columns)


def solution(mesh):
    in_specs = (P(None, "dom", None, None, "band"), P(None, "band"), P(None, "dom", None, None))
    out_specs = P(None, "dom", None, None, "band")
    return jax.shard_map(
        on_device, mesh=mesh, in_specs=in_specs, out_specs=out_specs, check_vma=False
    )
```

```python
import jax
import jax.numpy as jnp
from jax import lax
from jax.experimental import pallas as pl
from jax.experimental.pallas import tpu as pltpu
from jax.sharding import PartitionSpec as P

TILES_Y = 4


stencil_weights = (
    -5369.0 / 1800.0,
    12.0 / 7.0,
    -15.0 / 56.0,
    10.0 / 189.0,
    -1.0 / 112.0,
    2.0 / 1925.0,
    -1.0 / 16632.0,
)
inverse_spacing = 4.0
centre_shift = 20.0
spread_scale = 24.0

HALVES = 2
SIDE = 8
TAIL = 8
KERNEL_VMEM = 12 * 1024 * 1024

side_groups = [[h * SIDE + i for i in range(SIDE)] for h in range(HALVES)]
half_swap = [(b, (b + SIDE) % (HALVES * SIDE)) for b in range(HALVES * SIDE)]


def from_behind(value, axis, steps):
    count = lax.axis_size(axis)
    initial, last = (max(0, -steps), min(count, count - steps))
    return lax.ppermute(value, axis, [(source, source + steps) for source in range(initial, last)])


def along_y(value, steps):
    count = lax.axis_size("dom")
    pairs = [
        (source, source + steps)
        for source in range(count)
        if 0 <= source % TILES_Y + steps < TILES_Y
    ]
    return lax.ppermute(value, "dom", pairs)


def ramp(shape, axis):
    column = lax.broadcasted_iota(jnp.int32, shape, axis)
    return ((column * 159) & 255).astype(jnp.float32) / 256.0


def lateral_weights(extent, sources, place):
    factor = -0.5 * inverse_spacing / spread_scale
    shape = (extent * extent, sources)
    row = lax.broadcasted_iota(jnp.int32, shape, 0)
    first, second = place(lax.broadcasted_iota(jnp.int32, shape, 1))
    first = jnp.abs(row // extent - first)
    second = jnp.abs(row % extent - second)
    apart = jnp.where((first == 0) != (second == 0), first + second, 0)
    weights = jnp.zeros(shape, jnp.float32)
    for offset in range(1, len(stencil_weights)):
        weights = jnp.where(apart == offset, factor * stencil_weights[offset], weights)
    return weights


def store_terms(out_ref, matrix):
    rows = matrix.shape[0]
    for term in range(3):
        part = matrix.astype(jnp.bfloat16)
        out_ref[term * rows : (term + 1) * rows] = part
        matrix = matrix - part.astype(jnp.float32)


def along_planes(slab_ref, potential_ref, out_ref, first_ref, second_ref):
    reach = len(stencil_weights) - 1
    factor = -0.5 * inverse_spacing / spread_scale
    planes, points, columns = out_ref.shape
    extent = potential_ref.shape[1]
    cube = (planes * points // extent, extent, extent)
    across = lax.broadcasted_iota(jnp.int32, cube, 1) == lax.broadcasted_iota(jnp.int32, cube, 2)
    shift = jnp.where(across, jnp.broadcast_to(potential_ref[...][:, None, :], cube), 0.0)
    shift = jnp.sum(shift, axis=2, keepdims=True).reshape(planes, points, 1)
    shift = (shift - centre_shift) / spread_scale + 3.0 * factor * stencil_weights[0]
    width = 128
    for lane in range(0, columns, width):
        part = pl.ds(lane, width)
        for plane in range(planes):
            centre = slab_ref[plane + reach, :, part].astype(jnp.float32)
            total = shift[plane] * centre
            for offset in range(1, reach + 1):
                pair = slab_ref[plane + reach + offset, :, part].astype(jnp.float32)
                pair = pair + slab_ref[plane + reach - offset, :, part].astype(jnp.float32)
                total = total + factor * stencil_weights[offset] * pair
            out_ref[plane, :, part] = total
    halo = reach * extent

    def with_first(number):
        at = number // extent
        at = jnp.where(number >= points, at - extent - reach, at)
        at = jnp.where(number >= points + halo, at + extent, at)
        return at, number % extent

    def with_second(number):
        at = number % points
        return at // extent, at % extent + jnp.where(number < points, -extent, extent)

    store_terms(first_ref, lateral_weights(extent, first_ref.shape[1], with_first))
    store_terms(second_ref, lateral_weights(extent, second_ref.shape[1], with_second))


def lateral(
    partial_ref,
    middle_ref,
    below_first_ref,
    above_first_ref,
    below_second_ref,
    above_second_ref,
    first_ref,
    second_ref,
    out_ref,
):
    planes, points, columns = partial_ref.shape
    largest = jnp.zeros((points, columns), jnp.float32)
    for plane in range(planes):
        here = jnp.concatenate(
            [middle_ref[plane], below_first_ref[plane], above_first_ref[plane]], axis=0
        )
        there = jnp.concatenate([below_second_ref[plane], above_second_ref[plane]], axis=0)
        terms = jnp.dot(first_ref[...], here, preferred_element_type=jnp.float32)
        terms = terms + jnp.dot(second_ref[...], there, preferred_element_type=jnp.float32)
        total = partial_ref[plane] + (
            terms[:points] + (terms[points : 2 * points] + terms[2 * points :])
        )
        out_ref[plane * points : (plane + 1) * points] = total
        largest = jnp.maximum(largest, jnp.abs(total))
    largest = jnp.max(jnp.max(largest, axis=0, keepdims=True), axis=1, keepdims=True)
    largest = jnp.broadcast_to(largest, (TAIL, columns))
    exponent = jnp.floor(jnp.log2(jnp.maximum(largest, 2.0**-100))) - 13.0
    factor = jnp.exp2(ramp((TAIL, columns), 1) - exponent)[:1]
    for plane in range(planes):
        block = slice(plane * points, (plane + 1) * points)
        out_ref[block] = out_ref[block] * factor
    out_ref[planes * points :] = exponent


def filtered_code(slab, potential):
    reach = len(stencil_weights) - 1
    planes, extent_first, extent_second = potential.shape
    points, columns = slab.shape[1:]
    middle = slab[reach : reach + planes]
    below_second = along_y(middle, 1)
    above_second = along_y(middle, -1)
    below_first = from_behind(middle[:, (extent_first - reach) * extent_second :], "dom", TILES_Y)
    above_first = from_behind(middle[:, : reach * extent_second], "dom", -TILES_Y)
    vmem = pl.BlockSpec(memory_space=pltpu.VMEM)
    params = pltpu.CompilerParams(vmem_limit_bytes=KERNEL_VMEM)
    halo = reach * extent_second
    values = planes * points * columns
    partial, first, second = pl.pallas_call(
        along_planes,
        out_shape=(
            jax.ShapeDtypeStruct((planes, points, columns), jnp.float32),
            jax.ShapeDtypeStruct((3 * points, points + 2 * halo), jnp.bfloat16),
            jax.ShapeDtypeStruct((3 * points, 2 * points), jnp.bfloat16),
        ),
        in_specs=[vmem] * 2,
        out_specs=(vmem,) * 3,
        cost_estimate=pl.CostEstimate(
            flops=30 * values, bytes_accessed=2 * slab.size + 4 * values, transcendentals=0
        ),
        compiler_params=params,
        name="along_planes",
    )(slab, potential.reshape(planes * extent_first, extent_second))
    scaled = pl.pallas_call(
        lateral,
        out_shape=jax.ShapeDtypeStruct((planes * points + TAIL, columns), jnp.float32),
        in_specs=[vmem] * 8,
        out_specs=vmem,
        cost_estimate=pl.CostEstimate(
            flops=2 * planes * (first.size + second.size) * columns,
            bytes_accessed=16 * values,
            transcendentals=0,
        ),
        compiler_params=params,
        name="lateral",
    )(partial, middle, below_first, above_first, below_second, above_second, first, second)
    return scaled.astype(jnp.float16)


def spread(code):
    return lax.all_gather(code, "band", axis=0, axis_index_groups=side_groups)


def product(codes, matrix, rows, start=None):
    exponent = codes[:, rows : rows + 1].astype(jnp.float32)
    factor = jnp.exp2(exponent - ramp((1, 1, codes.shape[2]), 2))
    value = codes[:, :rows].astype(jnp.float32) * factor
    high = lax.reduce_precision(value, 8, 7)
    low = (value - high).astype(jnp.bfloat16)
    high = high.astype(jnp.bfloat16)
    dims = (((0, 2), (0, 1)), ((), ()))
    first = lax.dot_general(high, matrix, dims, preferred_element_type=jnp.float32)
    second = lax.dot_general(low, matrix, dims, preferred_element_type=jnp.float32)
    return (first if start is None else start + first) + second


def on_device(orbitals, rotation, potential):
    ghosted = orbitals.shape[0]
    extent_first = orbitals.shape[2]
    extent_second = orbitals.shape[3]
    columns = orbitals.shape[4]
    planes = potential.shape[0]
    new_columns = rotation.shape[1]
    rows = planes * extent_first * extent_second
    slab_local = orbitals.reshape(ghosted, extent_first * extent_second, columns)
    potential_local = potential.reshape(planes, extent_first, extent_second)

    code = filtered_code(slab_local, potential_local)
    rotation, code = lax.optimization_barrier((rotation, code))
    half = lax.axis_index("band") // SIDE
    halves = rotation.reshape(HALVES, SIDE, columns, new_columns)
    arrived = lax.ppermute(code, "band", half_swap)
    gathered = spread(code)
    own_matrix = lax.dynamic_index_in_dim(halves, half, 0, keepdims=False)
    own = product(gathered, own_matrix, rows)
    arrived, own = lax.optimization_barrier((arrived, own))
    gathered = spread(arrived)
    other_matrix = lax.dynamic_index_in_dim(halves, 1 - half, 0, keepdims=False)
    result = product(gathered, other_matrix, rows, own)
    return result.reshape(planes, 1, extent_first, extent_second, new_columns)


def solution(mesh):
    in_specs = (P(None, "dom", None, None, "band"), P(None, "band"), P(None, "dom", None, None))
    out_specs = P(None, "dom", None, None, "band")
    return jax.shard_map(
        on_device, mesh=mesh, in_specs=in_specs, out_specs=out_specs, check_vma=False
    )
```
